512 devices in a mesh: dp: 4 (over x), ctx: 128 (over y, z, core).
Axes of the slice: x: 4, y: 8, z: 8, core: 2. Of those that a mesh axis runs over, the one named last changes fastest.
Arguments:
- tokens: bfloat16 [4, 32768, 4096], P('dp', 'ctx'), may hold values from -6 to 6
- queries: bfloat16 [4, 32768, 2048], P('dp', 'ctx'), may hold values from -260 to 260, as said below
- kv_weight: bfloat16 [4096, 1024], P('ctx', 'dp'), may hold values from -0.09375 to 0.09375
- doc_blocks: int32 [4, 64], P('dp'), may hold values from 1 to 8, 256 in all within a row
- block_mask: int32 [4, 256, 7], P('dp'), may hold values 0 or 1
- plan: int32 [4, 256], P('dp'), may hold values from 0 to 255, as said below
Outputs:
- attended: bfloat16 [4, 32768, 2048], P('dp', 'ctx')
- stats: float32 [4, 16, 32768], P('dp', None, 'ctx')
The draws below stay inside these ranges and needn't reach their ends.
Inputs may be any that keep to these rules, and one draw needn't show every extreme that they name: queries of unit order, in some draws with a few rows far larger. `doc_blocks`: the documents of a pack in order, their lengths summing to 256. `block_mask`: entry [b, w] lets block b attend block b - w - 1 where that block is of the same document. plan[b] = ctx index * 2 + place; the slot lies on block b's own ctx index or on the one that differs from it in the lowest bit, and every slot is named by exactly one block.
All inputs are finite; a program needn't handle non-finite values.
Results may differ from the reference program's by a relative error of at most 0.012.
The reference program's roundings to bfloat16 on the way count: a program that leaves them out, or rounds other values in their place, can miss the bound.
Values may be sent and summed in bfloat16 or wider, within the bound.
A program may use at most 128 MiB of HBM per device.

```python
import math
import jax
import jax.numpy as jnp
import numpy as np
from jax import lax

D = 4096
HD = 128
QH = 16
KVH = 4
BLK = 128
MAXDOC = 8
BDEV = 2
PACKS = 4
NB = 256
PACK = 32768
NDOC = 64
KVW = 1024


def draw_queries(key, part):
    shape = (PACKS, NB * BLK, QH * HD)
    first = jax.random.fold_in(key, 0)
    return jnp.clip(jax.random.normal(first, shape, jnp.float32), -4.0, 4.0).astype(jnp.bfloat16)


def draw_plan(key, part):
    group = 2 * BDEV
    count = NB // group

    def one_pack(pack_key):
        scores = jax.random.randint(pack_key, (count, group), 0, 1 << 20)
        scores = scores * group + jnp.arange(group, dtype=jnp.int32)[None, :]
        order = jnp.argsort(scores, axis=1).astype(jnp.int32)
        offsets = (jnp.arange(count, dtype=jnp.int32) * group)[:, None]
        return (offsets + order).reshape(NB).astype(jnp.int32)
    return jax.vmap(one_pack)(jax.random.split(key, PACKS))


def with_ends(drawn, stream_key, least, high):
    dims = drawn.shape
    spot = [jax.random.randint(jax.random.fold_in(stream_key, axis), (), 0, dims[axis]) for axis in range(len(dims))]
    drawn = drawn.at[tuple(spot)].set(least)
    longest = dims.index(max(dims))
    spot[longest] = (spot[longest] + 1) % dims[longest]
    return drawn.at[tuple(spot)].set(high)


def block_levels(rng, dims, cuts, low, largest):
    def one(dim, blocks):
        draws = jax.random.uniform(jax.random.fold_in(jax.random.fold_in(rng, 6), dim), (blocks,), jnp.float32, low / len(cuts), largest / len(cuts))
        return jnp.repeat(jnp.exp(draws), dims[dim] // blocks).reshape((-1,) + (1,) * (len(dims) - dim - 1))

    factor_of = one(*cuts[0])
    for cut in cuts[1:]:
        factor_of = factor_of * one(*cut)
    return factor_of


def length_profile(number_of, total, reach, lean):
    loads = [(1 << 20) // math.isqrt(grade ** lean) + 1 for grade in range(2, number_of + 1)]
    rest, holding = total - reach - (number_of - 1), [1] * (number_of - 1)
    while rest > 0:
        movable = [i for i in range(number_of - 1) if holding[i] < reach]
        pool, budget = sum([loads[i] for i in movable]), rest
        for i in movable:
            more = min(reach - holding[i], max(1, budget * loads[i] // pool), rest)
            holding[i] = holding[i] + more
            rest = rest - more
    return np.array([reach] + holding)


def ragged_sizes(stream_key, amount, total, limit, lean):
    if amount == 2:
        one = jax.random.randint(stream_key, (), max(1, total - limit), min(limit, total - 1) + 1)
        return jnp.stack([one, total - one])
    lengths = jnp.asarray(length_profile(amount, total, limit, lean), jnp.int32)
    twos = (amount - 1) // 2
    giver, sink = lengths[1:1 + 2 * twos:2], lengths[2:2 + 2 * twos:2]
    room = jnp.minimum(giver - 1, limit - sink)
    passed = jax.random.randint(jax.random.fold_in(stream_key, 1), (twos,), 0, 1 << 20) % (room + 1)
    lengths = lengths.at[1:1 + 2 * twos:2].set(giver - passed).at[2:2 + 2 * twos:2].set(sink + passed)
    return lengths[jax.random.permutation(jax.random.fold_in(stream_key, 2), amount)]


def normal_values(own_key, dims, scale, limit, cuts=(), held_as=jnp.bfloat16):
    gain = block_levels(own_key, dims, cuts, -0.22, 0.18) if cuts else 1.0
    values = jax.random.normal(own_key, dims, jnp.float32) * scale * gain
    return jnp.minimum(jnp.maximum(values, -limit), limit).astype(held_as)


def setup_inputs(seed: int = 0) -> dict:
    seeds = jax.random.split(jax.random.key(seed), 7)
    tokens = normal_values(seeds[0], (PACKS, PACK, D), 1.0, 6.0, ((0, 4), (1, 128)))
    queries = draw_queries(jax.random.fold_in(seeds[6], 71), 0)
    kv_weight = normal_values(seeds[2], (D, KVW), D ** -0.5, 0.09375, ((0, 128), (1, 4)))
    doc_blocks = jax.vmap(lambda own: ragged_sizes(own, NDOC, NB, MAXDOC, 2))(jax.random.split(seeds[3], PACKS)).reshape((PACKS, NDOC)).astype(jnp.int32)
    block_mask = with_ends((jax.random.randint(seeds[4], (PACKS, NB, MAXDOC - 1), 0, 4) < 3).astype(jnp.int32), jax.random.fold_in(seeds[4], 1), 0, 1)
    plan = draw_plan(jax.random.fold_in(seeds[6], 71), 0)
    return {"tokens": tokens, "queries": queries, "kv_weight": kv_weight, "doc_blocks": doc_blocks, "block_mask": block_mask, "plan": plan}


def document_of_blocks(doc_blocks):
    ends = jnp.cumsum(doc_blocks).astype(jnp.int32)
    blocks = jnp.arange(NB, dtype=jnp.int32)
    return lax.optimization_barrier(jnp.sum((blocks[:, None] >= ends[None, :]).astype(jnp.int32), axis=1)).astype(jnp.int32)

def attend_pack(tokens, queries, kv_weight, doc_blocks, block_mask, plan):
    group = QH // KVH
    width = 2 * KVH * HD
    pairs = jnp.dot(tokens, kv_weight, preferred_element_type=jnp.float32).astype(jnp.bfloat16)
    pairs = pairs.reshape(NB, BLK, width)
    padded = jnp.concatenate([jnp.zeros((MAXDOC - 1, BLK, width), jnp.bfloat16), pairs], axis=0)
    documents = document_of_blocks(doc_blocks)
    padded_docs = jnp.concatenate([jnp.full((MAXDOC - 1,), -1, jnp.int32), documents])
    heads = queries.reshape(NB, BLK, KVH, group, HD)
    places = jnp.arange(BLK, dtype=jnp.int32)
    causal = places[None, :] <= places[:, None]
    last = jnp.arange(MAXDOC, dtype=jnp.int32) == MAXDOC - 1
    token_keep = jnp.logical_or(jnp.logical_not(last)[:, None, None], causal[None])
    scale = 1.0 / math.sqrt(HD)

    def one_block(index):
        window = lax.dynamic_slice_in_dim(padded, index, MAXDOC, 0)
        window_docs = lax.dynamic_slice_in_dim(padded_docs, index, MAXDOC, 0)
        gates = jnp.concatenate([block_mask[index][::-1], jnp.ones((1,), jnp.int32)])
        allowed = (window_docs == documents[index]) & (gates == 1)
        keys = window[:, :, :KVH * HD].reshape(MAXDOC * BLK, KVH, HD).astype(jnp.float32)
        values = window[:, :, KVH * HD:].reshape(MAXDOC * BLK, KVH, HD).astype(jnp.float32)
        query = heads[index].astype(jnp.float32)
        scores = jnp.einsum('ikgd,lkd->kgil', query, keys) * scale
        keep = (allowed[:, None, None] & token_keep).transpose(1, 0, 2).reshape(BLK, MAXDOC * BLK)
        scores = jnp.where(keep[None, None], scores, -jnp.inf)
        rowmax = lax.optimization_barrier(jnp.max(scores, axis=-1, keepdims=True))
        weights = jnp.exp(scores - rowmax)
        total = lax.optimization_barrier(jnp.sum(weights, axis=-1))
        rounded = lax.optimization_barrier(weights.astype(jnp.bfloat16)).astype(jnp.float32)
        summed = jnp.einsum('kgil,lkd->kgid', rounded, values)
        out = (summed / total[..., None]).transpose(2, 0, 1, 3).reshape(BLK, QH * HD).astype(jnp.bfloat16)
        stats = (rowmax[..., 0] + jnp.log(total)).reshape(QH, BLK)
        return (out, stats)
    outs, stats = lax.map(one_block, jnp.arange(NB, dtype=jnp.int32))
    placed = jnp.zeros_like(stats).at[plan].set(stats)
    return (outs.reshape(NB * BLK, QH * HD), placed.transpose(1, 0, 2).reshape(QH, NB * BLK))

def reference(tokens, queries, kv_weight, doc_blocks, block_mask, plan):
    results = [attend_pack(tokens[pack], queries[pack], kv_weight, doc_blocks[pack], block_mask[pack], plan[pack]) for pack in range(PACKS)]
    return (jnp.stack([item[0] for item in results]), jnp.stack([item[1] for item in results]))
```

```python
import functools
import math

import jax
import jax.numpy as jnp
from jax import lax
from jax.experimental import pallas as pl
from jax.experimental.pallas import tpu as pltpu
from jax.sharding import PartitionSpec as P

HD = 128
QH = 16
KVH = 4
BLK = 128
MAXDOC = 8
GROUP = QH // KVH
CHIP_BLOCKS = 4
BACK = MAXDOC - 1
WINDOW = BACK + CHIP_BLOCKS
NEAR = BACK - CHIP_BLOCKS
HALF = QH * HD // 2
KW = KVH * HD // 2
SCALE2 = math.log2(math.e) / math.sqrt(HD)
LN2 = math.log(2.0)
MESH = pl.DeviceIdType.MESH
BF16 = jnp.bfloat16
F32 = jnp.float32
NT = (((1,), (1,)), ((), ()))


def kernel(
    n,
    tok_in,
    q_in,
    w_in,
    docs_ref,
    mask_ref,
    plan_ref,
    out_ref,
    stats_ref,
    tok,
    wbuf,
    q,
    kbuf,
    vbuf,
    prod,
    o,
    acc_s,
    m_s,
    l_s,
    lse_t,
    lse_b,
    picked,
    bias,
    loc_sem,
    tok_sem,
    q_sem,
    wx_send,
    wx_recv,
    s1_send,
    s1_recv,
    s2_send,
    s2_recv,
    kv_send,
    kv_recv,
    out_send,
    out_recv,
    st_send,
    st_recv,
):
    x = lax.axis_index("dp")
    ctx = lax.axis_index("ctx")
    chips = n * n
    core = lax.rem(ctx, 2)
    chip = lax.div(ctx, 2)
    z = lax.rem(chip, n)
    y = lax.div(chip, n)
    other = 1 - core
    partner = chip * 2 + other
    on_y = core == 0
    first_pos = jnp.where(on_y, y, z)
    ring_pos = jnp.where(on_y, z, y)

    def first_peer(step):
        pos = lax.rem(first_pos + step, n)
        return jnp.where(on_y, pos * n + z, y * n + pos) * 2 + core

    def ring_peer(step):
        pos = lax.rem(ring_pos + step, n)
        return jnp.where(on_y, y * n + pos, pos * n + z) * 2 + core

    after = lax.rem(chip + 1, chips) * 2 + core
    before = lax.rem(chip + chips - 1, chips) * 2 + core

    local = [
        pltpu.make_async_copy(tok_in.at[0], tok.at[pl.ds(core * 256, 256)], loc_sem.at[0]),
        pltpu.make_async_copy(
            q_in.at[0, :, pl.ds(pl.multiple_of(core * HALF, HALF), HALF)],
            q.at[pl.ds(core * 256, 256)],
            loc_sem.at[1],
        ),
    ]
    for copy in local:
        copy.start()

    barrier = pltpu.get_barrier_semaphore()
    peers = [(x, partner)]
    for step in range(1, 4):
        other_x = lax.rem(x + step, 4)
        peers += [(other_x, ctx), (other_x, partner)]
    peers += [(x, first_peer(step)) for step in range(1, n)]
    peers += [(x, ring_peer(1)), (x, ring_peer(n - 1)), (x, after), (x, before)]
    for peer in peers:
        pl.semaphore_signal(barrier, inc=1, device_id=peer, device_id_type=MESH)
    pl.semaphore_wait(barrier, len(peers))

    def remote(src, dst, send, recv, device):
        return pltpu.make_async_remote_copy(
            src_ref=src, dst_ref=dst, send_sem=send, recv_sem=recv, device_id=device, device_id_type=MESH
        )

    dest_core = lax.rem(x, 2)
    part = lax.div(x, 2)
    dest_a = jnp.where(dest_core == 0, z, y)
    dest_b = jnp.where(dest_core == 0, y, z)
    slot = wbuf.at[
        dest_a,
        dest_b,
        pl.ds(pl.multiple_of(core * 32, 32), 32),
        pl.ds(pl.multiple_of(part * KW, KW), KW),
    ]
    place = part * 2 + core
    dest_ctx = chip * 2 + dest_core
    piece_sends = [
        remote(w_in, slot, wx_send.at[step], wx_recv.at[place], (lax.rem(x + step, 4), dest_ctx))
        for step in range(1, 4)
    ]
    for copy in piece_sends:
        copy.start()
    piece_over = remote(w_in, slot, wx_send.at[0], wx_recv.at[place], (x, partner))

    @pl.when(dest_core == core)
    def _():
        pltpu.make_async_copy(w_in, slot, wx_recv.at[place]).start()

    @pl.when(dest_core != core)
    def _():
        piece_over.start()

    tok_send = remote(
        tok_in.at[0], tok.at[pl.ds(core * 256, 256)], tok_sem.at[0], tok_sem.at[1], (x, partner)
    )
    q_send = remote(
        q_in.at[0, :, pl.ds(pl.multiple_of(other * HALF, HALF), HALF)],
        q.at[pl.ds(core * 256, 256)],
        q_sem.at[0],
        q_sem.at[1],
        (x, partner),
    )
    mine = wbuf.at[ring_pos, first_pos]
    for k in range(4):
        quarter = wbuf.at[ring_pos, first_pos, pl.ds((k % 2) * 32, 32), pl.ds((k // 2) * KW, KW)]
        pltpu.make_async_copy(quarter, quarter, wx_recv.at[k]).wait()
    first_sends = [
        remote(mine, mine, s1_send.at[step], s1_recv.at[step], (x, first_peer(step)))
        for step in range(1, n)
    ]
    for copy in first_sends:
        copy.start()
    tok_send.start()
    q_send.start()

    base = chip * CHIP_BLOCKS - BACK

    def count(j, state):
        end = state[0] + docs_ref[0, j]
        return (end,) + tuple(
            state[1 + b] + jnp.where(base + b >= end, 1, 0) for b in range(WINDOW)
        )

    zero = jnp.int32(0)
    document = lax.fori_loop(0, docs_ref.shape[1], count, (zero,) * (WINDOW + 1))[1:]
    for i in range(CHIP_BLOCKS):
        for s in range(BACK):
            key = i + s
            keep = jnp.logical_and(document[key] == document[i + BACK], base + key >= 0)
            keep = jnp.logical_and(keep, mask_ref[BACK - s - 1, chip * CHIP_BLOCKS + i] == 1)
            bias[i * MAXDOC + s] = jnp.where(keep, jnp.float32(0.0), jnp.float32(-jnp.inf))

    for step in range(1, n):
        source = lax.rem(first_pos + n - step, n)
        got = wbuf.at[ring_pos, source]
        pltpu.make_async_copy(got, got, s1_recv.at[step]).wait()

    half = n // 2
    steps = n // 2

    def ring_copy(way, k, h):
        shift = n - (k - 1) if way == 0 else k - 1
        chunk = wbuf.at[lax.rem(ring_pos + shift, n), pl.ds(h * half, half)]
        to = ring_peer(1) if way == 0 else ring_peer(n - 1)
        return remote(chunk, chunk, s2_send.at[way, k, h], s2_recv.at[way, k, h], (x, to))

    def ring_got(way, k, h):
        shift = n - k if way == 0 else k
        chunk = wbuf.at[lax.rem(ring_pos + shift, n), pl.ds(h * half, half)]
        pltpu.make_async_copy(chunk, chunk, s2_recv.at[way, k, h]).wait()

    ring_sends = []

    def ring_start(way, k, h):
        if k < steps or h == way:
            copy = ring_copy(way, k, h)
            copy.start()
            ring_sends.append(copy)

    order = ((0, 0), (1, 1), (0, 1), (1, 0))
    for k in range(1, steps + 1):
        for way, h in order:
            if k > 1:
                ring_got(way, k - 1, h)
            ring_start(way, k, h)
    ring_got(0, steps, 0)
    ring_got(1, steps, 1)

    for copy in local:
        copy.wait()
    tok_send.wait_recv()
    q_send.wait_recv()

    def project(column, dest):
        prod[...] = jnp.zeros_like(prod)

        @pl.loop(0, n)
        def _(k):
            rows = [
                wbuf[
                    jnp.where(on_y, j, k),
                    jnp.where(on_y, k, j),
                    :,
                    pl.ds(column, KW),
                ]
                for j in range(n)
            ]
            taken = tok[:, pl.ds(pl.multiple_of(k * (64 * n), 64 * n), 64 * n)]
            prod[...] += jnp.dot(taken, jnp.concatenate(rows, axis=0), preferred_element_type=F32)

        dest[pl.ds(BACK * BLK, CHIP_BLOCKS * BLK), :] = prod[...].astype(BF16)

    kv_sends = []

    def pass_on(index, buf, src, dst, count):
        copy = remote(
            buf.at[pl.ds(src * BLK, count * BLK)],
            buf.at[pl.ds(dst * BLK, count * BLK)],
            kv_send.at[index],
            kv_recv.at[index],
            (x, after),
        )
        copy.start()
        kv_sends.append(copy)

    project(0, kbuf)
    pass_on(0, kbuf, BACK, NEAR, CHIP_BLOCKS)
    project(KW, vbuf)
    pass_on(1, vbuf, BACK, NEAR, CHIP_BLOCKS)
    kv_sends[0].wait_recv()
    pass_on(2, kbuf, NEAR + 1, 0, NEAR)
    kv_sends[1].wait_recv()
    pass_on(3, vbuf, NEAR + 1, 0, NEAR)

    causal = (
        lax.broadcasted_iota(jnp.int32, (GROUP * BLK, BLK), 1)
        <= lax.broadcasted_iota(jnp.int32, (GROUP * BLK, BLK), 0) % BLK
    )
    lane = lax.broadcasted_iota(jnp.int32, (BLK, BLK), 1)

    def scores(i, g, low, high):
        rows = q[pl.ds(i * BLK, BLK), pl.ds(pl.multiple_of(g * (GROUP * HD), GROUP * HD), GROUP * HD)]
        heads = jnp.concatenate([rows[:, h * HD : (h + 1) * HD] for h in range(GROUP)], axis=0)
        columns = pl.ds(pl.multiple_of(g * HD, HD), HD)
        keys = kbuf[pl.ds(low * BLK, (high - low) * BLK), columns]
        table = lax.dot_general(heads, keys, NT, preferred_element_type=F32)
        tiles = []
        for key in range(low, high):
            tile = table[:, (key - low) * BLK : (key - low + 1) * BLK] * SCALE2
            if key == i + BACK:
                tile = jnp.where(causal, tile, -jnp.inf)
            else:
                tile = tile + bias[i * MAXDOC + key - i]
            tiles.append(tile)
        return tiles

    def weigh(tiles, top, g, low, high):
        weights = [jnp.exp2(tile - top) for tile in tiles]
        total = functools.reduce(jnp.add, weights)
        total = jnp.sum(total, axis=1, keepdims=True)
        columns = pl.ds(pl.multiple_of(g * HD, HD), HD)
        values = vbuf[pl.ds(low * BLK, (high - low) * BLK), columns]
        packed = jnp.concatenate([w.astype(BF16) for w in weights], axis=1)
        return total, jnp.dot(packed, values, preferred_element_type=F32)

    def finish(i, g, top, total, summed):
        result = (summed / total).astype(BF16)
        lse = (top + jnp.log2(total)) * LN2
        for h in range(GROUP):
            column = pl.multiple_of(g * (GROUP * HD) + h * HD, HD)
            o[pl.ds(i * BLK, BLK), pl.ds(column, HD)] = result[h * BLK : (h + 1) * BLK]
            lse_t[i] = jnp.where(lane == g * GROUP + h, lse[h * BLK : (h + 1) * BLK], lse_t[i])

    def highest(tiles):
        return jnp.max(functools.reduce(jnp.maximum, tiles), axis=1, keepdims=True)

    lse_t[...] = jnp.zeros_like(lse_t)

    def near_part(i):
        @pl.loop(0, KVH // 2)
        def _(g):
            low, high = NEAR, i + BACK + 1
            tiles = scores(i, g, low, high)
            top = highest(tiles)
            total, summed = weigh(tiles, top, g, low, high)
            if i == CHIP_BLOCKS - 1:
                finish(i, g, top, total, summed)
            else:
                acc_s[i, g] = summed
                m_s[i, g] = top
                l_s[i, g] = total

    def far_part(i):
        @pl.loop(0, KVH // 2)
        def _(g):
            low, high = i, NEAR
            tiles = scores(i, g, low, high)
            top = jnp.maximum(highest(tiles), m_s[i, g])
            keep = jnp.exp2(m_s[i, g] - top)
            total, summed = weigh(tiles, top, g, low, high)
            finish(i, g, top, total + l_s[i, g] * keep, summed + acc_s[i, g] * keep)

    def out_copy(i):
        rows = pl.ds((i % 2) * BLK, BLK)
        columns = pl.ds(pl.multiple_of(core * HALF, HALF), HALF)
        return o.at[pl.ds(i * BLK, BLK)], out_ref.at[0, rows, columns]

    def hand_out(i):
        lse_b[i] = lse_t[i].T[: QH // 2]
        src, dst = out_copy(i)

        @pl.when(core == i // 2)
        def _():
            pltpu.make_async_copy(src, dst, loc_sem.at[2 + i]).start()

        @pl.when(core != i // 2)
        def _():
            remote(src, dst, out_send.at[i % 2], out_recv.at[i % 2], (x, partner)).start()

    for i in range(CHIP_BLOCKS - 1, -1, -1):
        near_part(i)
    hand_out(CHIP_BLOCKS - 1)
    kv_sends[2].wait_recv()
    kv_sends[3].wait_recv()
    for i in (2, 0, 1):
        far_part(i)
        hand_out(i)

    for t in range(2):
        for j in range(2):
            slot_id = chip * CHIP_BLOCKS + t * 2 + j
            chosen = jnp.zeros((QH // 2, BLK), F32)
            for i in range(CHIP_BLOCKS):
                here = plan_ref[0, chip * CHIP_BLOCKS + i] == slot_id
                chosen += jnp.where(here, jnp.float32(1.0), jnp.float32(0.0)) * lse_b[i]
            picked[t, :, pl.ds(j * BLK, BLK)] = chosen
    stat_rows = stats_ref.at[0, pl.ds(pl.multiple_of(core * (QH // 2), QH // 2), QH // 2)]
    keep_stats = pltpu.make_async_copy(picked.at[core], stat_rows, loc_sem.at[6])
    give_stats = remote(picked.at[other], stat_rows, st_send, st_recv, (x, partner))
    keep_stats.start()
    give_stats.start()

    for i in range(CHIP_BLOCKS):
        src, dst = out_copy(i)

        @pl.when(core == i // 2)
        def _():
            pltpu.make_async_copy(src, dst, loc_sem.at[2 + i]).wait()

        @pl.when(core != i // 2)
        def _():
            copy = remote(src, dst, out_send.at[i % 2], out_recv.at[i % 2], (x, partner))
            copy.wait_send()
            copy.wait_recv()

    keep_stats.wait()
    give_stats.wait_send()
    give_stats.wait_recv()
    for copy in piece_sends + first_sends + ring_sends + kv_sends:
        copy.wait_send()
    tok_send.wait_send()
    q_send.wait_send()

    @pl.when(dest_core != core)
    def _():
        piece_over.wait_send()


def body(n, tokens, queries, kv_weight, doc_blocks, block_mask, plan):
    wide = 64 * n * n
    smem = pl.BlockSpec(memory_space=pltpu.SMEM)
    hbm = pl.BlockSpec(memory_space=pl.ANY)
    dma = pltpu.SemaphoreType.DMA
    parts = KVH // 2
    rows = CHIP_BLOCKS * BLK
    early = CHIP_BLOCKS - 1
    return pl.pallas_call(
        functools.partial(kernel, n),
        out_shape=(
            jax.ShapeDtypeStruct(queries.shape, BF16),
            jax.ShapeDtypeStruct((1, QH, tokens.shape[1]), F32),
        ),
        in_specs=[hbm, hbm, hbm, smem, smem, smem],
        out_specs=(hbm, hbm),
        scratch_shapes=[
            pltpu.VMEM((rows, wide), BF16),
            pltpu.VMEM((n, n, 64, 2 * KW), BF16),
            pltpu.VMEM((rows, HALF), BF16),
            pltpu.VMEM((WINDOW * BLK, KW), BF16),
            pltpu.VMEM((WINDOW * BLK, KW), BF16),
            pltpu.VMEM((rows, KW), F32),
            pltpu.VMEM((rows, HALF), BF16),
            pltpu.VMEM((early, parts, GROUP * BLK, HD), F32),
            pltpu.VMEM((early, parts, GROUP * BLK, 1), F32),
            pltpu.VMEM((early, parts, GROUP * BLK, 1), F32),
            pltpu.VMEM((CHIP_BLOCKS, BLK, BLK), F32),
            pltpu.VMEM((CHIP_BLOCKS, QH // 2, BLK), F32),
            pltpu.VMEM((2, QH // 2, 2 * BLK), F32),
            pltpu.SMEM((CHIP_BLOCKS * MAXDOC,), F32),
            dma((7,)),
            dma((2,)),
            dma((2,)),
            dma((4,)),
            dma((4,)),
            dma((n,)),
            dma((n,)),
            dma((2, n // 2 + 1, 2)),
            dma((2, n // 2 + 1, 2)),
            dma((4,)),
            dma((4,)),
            dma((2,)),
            dma((2,)),
            dma,
            dma,
        ],
        compiler_params=pltpu.CompilerParams(
            collective_id=0, has_side_effects=True, vmem_limit_bytes=50 * 1024 * 1024
        ),
    )(tokens, queries, kv_weight, doc_blocks, block_mask[0].T, plan)


def solution(mesh):
    in_specs = (
        P("dp", "ctx", None),
        P("dp", "ctx", None),
        P("ctx", "dp"),
        P("dp", None),
        P("dp", None, None),
        P("dp", None),
    )
    out_specs = (P("dp", "ctx", None), P("dp", None, "ctx"))
    n = math.isqrt(mesh.shape["ctx"] // 2)
    return jax.shard_map(
        functools.partial(body, n), mesh=mesh, in_specs=in_specs, out_specs=out_specs, check_vma=False
    )
```

```python
import functools
import math

import jax
import jax.numpy as jnp
from jax import lax
from jax.experimental import pallas as pl
from jax.experimental.pallas import tpu as pltpu
from jax.sharding import PartitionSpec as P

HD = 128
QH = 16
KVH = 4
BLK = 128
MAXDOC = 8
GROUP = QH // KVH
CHIP_BLOCKS = 4
BACK = MAXDOC - 1
WINDOW = BACK + CHIP_BLOCKS
NEAR = BACK - CHIP_BLOCKS
HALF = QH * HD // 2
KW = KVH * HD // 2
SCALE2 = math.log2(math.e) / math.sqrt(HD)
LN2 = math.log(2.0)
MESH = pl.DeviceIdType.MESH
BF16 = jnp.bfloat16
F32 = jnp.float32
NT = (((1,), (1,)), ((), ()))


def kernel(
    n,
    tok_in,
    q_in,
    w_in,
    docs_in,
    mask_in,
    plan_in,
    out_ref,
    stats_ref,
    tok,
    wbuf,
    q,
    kv,
    prod,
    o,
    acc_s,
    m_s,
    l_s,
    lse_b,
    picked,
    docs,
    mask,
    plan,
    bias,
    loc_sem,
    tok_sem,
    q_sem,
    wx_send,
    wx_recv,
    s1_send,
    s1_recv,
    s2_send,
    s2_recv,
    kv_send,
    kv_recv,
    out_loc,
    out_send,
    out_recv,
    st_send,
    st_recv,
):
    x = lax.axis_index("dp")
    ctx = lax.axis_index("ctx")
    chips = n * n
    half = n // 2
    core = lax.rem(ctx, 2)
    chip = lax.div(ctx, 2)
    z = lax.rem(chip, n)
    y = lax.div(chip, n)
    other = 1 - core
    partner = chip * 2 + other
    on_y = core == 0
    first_pos = jnp.where(on_y, y, z)
    ring_pos = jnp.where(on_y, z, y)

    def first_peer(step):
        pos = lax.rem(first_pos + step, n)
        return jnp.where(on_y, pos * n + z, y * n + pos) * 2 + core

    def ring_peer(step):
        pos = lax.rem(ring_pos + step, n)
        return jnp.where(on_y, y * n + pos, pos * n + z) * 2 + core

    after = lax.rem(chip + 1, chips) * 2 + core
    before = lax.rem(chip + chips - 1, chips) * 2 + core

    def remote(src, dst, send, recv, device):
        return pltpu.make_async_remote_copy(
            src_ref=src, dst_ref=dst, send_sem=send, recv_sem=recv, device_id=device, device_id_type=MESH
        )

    def arrived(ref, sem):
        pltpu.make_async_copy(ref, ref, sem).wait()

    barrier = pltpu.get_barrier_semaphore()
    peers = [(x, partner)]
    for step in range(1, 4):
        other_x = lax.rem(x + step, 4)
        peers += [(other_x, ctx), (other_x, partner)]
    peers += [(x, first_peer(step)) for step in range(1, n)]
    peers += [(x, ring_peer(1)), (x, ring_peer(n - 1)), (x, after), (x, before)]
    for peer in peers:
        pl.semaphore_signal(barrier, inc=1, device_id=peer, device_id_type=MESH)

    local = [
        pltpu.make_async_copy(tok_in.at[0], tok.at[pl.ds(core * 256, 256)], loc_sem.at[0]),
        pltpu.make_async_copy(
            q_in.at[0, :, pl.ds(pl.multiple_of(core * HALF, HALF), HALF)],
            q.at[pl.ds(core * 256, 256)],
            loc_sem.at[1],
        ),
    ]
    tables = [
        pltpu.make_async_copy(docs_in, docs, loc_sem.at[2]),
        pltpu.make_async_copy(mask_in, mask, loc_sem.at[3]),
        pltpu.make_async_copy(plan_in, plan, loc_sem.at[4]),
    ]
    for copy in local + tables:
        copy.start()
    pl.semaphore_wait(barrier, len(peers))

    dest_core = lax.rem(x, 2)
    part = lax.div(x, 2)
    dest_a = jnp.where(dest_core == 0, z, y)
    dest_b = jnp.where(dest_core == 0, y, z)
    slot = wbuf.at[
        dest_a,
        dest_b,
        pl.ds(pl.multiple_of(core * 32, 32), 32),
        pl.ds(pl.multiple_of(part * KW, KW), KW),
    ]
    place = part * 2 + core
    dest_ctx = chip * 2 + dest_core
    piece_sends = [
        remote(w_in, slot, wx_send.at[step], wx_recv.at[place], (lax.rem(x + step, 4), dest_ctx))
        for step in (2, 1, 3)
    ]
    for copy in piece_sends:
        copy.start()
    piece_over = remote(w_in, slot, wx_send.at[0], wx_recv.at[place], (x, partner))

    @pl.when(dest_core == core)
    def _():
        pltpu.make_async_copy(w_in, slot, wx_recv.at[place]).start()

    @pl.when(dest_core != core)
    def _():
        piece_over.start()

    tok_send = remote(
        tok_in.at[0], tok.at[pl.ds(core * 256, 256)], tok_sem.at[0], tok_sem.at[1], (x, partner)
    )
    q_send = remote(
        q_in.at[0, :, pl.ds(pl.multiple_of(other * HALF, HALF), HALF)],
        q.at[pl.ds(core * 256, 256)],
        q_sem.at[0],
        q_sem.at[1],
        (x, partner),
    )
    for k in range(4):
        arrived(
            wbuf.at[ring_pos, first_pos, pl.ds((k % 2) * 32, 32), pl.ds((k // 2) * KW, KW)],
            wx_recv.at[k],
        )

    steps = half

    def ring_copy(way, k, h):
        row = n - (k - 1) if way == 0 else k - 1
        chunk = wbuf.at[lax.rem(ring_pos + row, n), pl.ds(h * half, half)]
        to = ring_peer(1) if way == 0 else ring_peer(n - 1)
        return remote(chunk, chunk, s2_send.at[way, k, h], s2_recv.at[way, k, h], (x, to))

    def ring_got(way, k, h):
        row = n - k if way == 0 else k
        arrived(wbuf.at[lax.rem(ring_pos + row, n), pl.ds(h * half, half)], s2_recv.at[way, k, h])

    sends = []

    def start(copy):
        copy.start()
        sends.append(copy)

    def ring_start(way, k, h):
        if k < steps or h == way:
            start(ring_copy(way, k, h))

    def pair_operands(m):
        taken, rows = [], []
        for j in range(n):
            row = 2 * m + j // half
            pair = 2 * (j % half)
            rows.append(wbuf[jnp.where(on_y, 2 * m, row), jnp.where(on_y, j, pair)])
            rows.append(wbuf[jnp.where(on_y, 2 * m + 1, row), jnp.where(on_y, j, pair + 1)])
            column = jnp.where(on_y, j * n + 2 * m, row * n + pair) * 64
            taken.append(tok[:, pl.ds(pl.multiple_of(column, 128), 128)])
        rows = jnp.concatenate(rows, axis=0)
        return jnp.concatenate(taken, axis=1), rows

    def head_columns(rows, g):
        return jnp.concatenate(
            [rows[:, g * HD : (g + 1) * HD], rows[:, KW + g * HD : KW + (g + 1) * HD]], axis=1
        )

    def project(m, fresh):
        taken, rows = pair_operands(m)
        for g in range(KVH // 2):
            part_sum = jnp.dot(taken, head_columns(rows, g), preferred_element_type=F32)
            prod[g] = part_sum if fresh else prod[g] + part_sum

    pairs = half
    even = lax.rem(ring_pos, 2) == 0
    middle = lax.div(ring_pos, 2)
    near_side = jnp.where(even, pairs - 1, 1)
    far_side = jnp.where(even, 1, pairs - 1)
    units = {
        2: [middle],
        4: [middle, lax.rem(middle + 1, pairs)],
        8: [
            middle,
            lax.rem(middle + near_side, pairs),
            lax.rem(middle + far_side, pairs),
            lax.rem(middle + 2, pairs),
        ],
    }[n]

    mine = wbuf.at[ring_pos, first_pos]
    for step in sorted(range(1, n), key=lambda step: min(step, n - step), reverse=True):
        start(remote(mine, mine, s1_send.at[step], s1_recv.at[step], (x, first_peer(step))))
    tok_send.start()
    q_send.start()

    for copy in tables:
        copy.wait()
    base = chip * CHIP_BLOCKS - BACK

    def count(j, state):
        end = state[0] + docs[0, j]
        return (end,) + tuple(
            state[1 + b] + jnp.where(base + b >= end, 1, 0) for b in range(WINDOW)
        )

    zero = jnp.int32(0)
    document = lax.fori_loop(0, docs.shape[1], count, (zero,) * (WINDOW + 1))[1:]
    for i in range(CHIP_BLOCKS):
        for s in range(BACK):
            key = i + s
            keep = jnp.logical_and(document[key] == document[i + BACK], base + key >= 0)
            gate = mask[BACK - s - 1, 0, chip * CHIP_BLOCKS + i] == 1
            keep = jnp.logical_and(keep, gate)
            bias[i * MAXDOC + s] = jnp.where(
                keep, jnp.float32(0.0), jnp.float32(-jnp.inf)
            )

    for step in range(1, n):
        source = lax.rem(first_pos + n - step, n)
        arrived(wbuf.at[ring_pos, source], s1_recv.at[step])

    order = ((0, 0), (1, 1), (0, 1), (1, 0))
    for k in range(1, steps + 1):
        for way, h in order:
            if k > 1:
                ring_got(way, k - 1, h)
            ring_start(way, k, h)
    ring_got(0, steps, 0)
    ring_got(1, steps, 1)
    local[0].wait()
    tok_send.wait_recv()
    for unit in range(steps - 1):
        project(units[unit], unit == 0)

    def passed(stage, g):
        if stage == 0:
            src, dst, count = BACK, NEAR, CHIP_BLOCKS
        else:
            src, dst, count = NEAR + 1, 0, NEAR
        return remote(
            kv.at[g, pl.ds(src, count)],
            kv.at[g, pl.ds(dst, count)],
            kv_send.at[stage, g],
            kv_recv.at[stage, g],
            (x, after),
        )

    taken, rows = pair_operands(units[-1])
    for g in range(KVH // 2):
        pair_kv = jnp.dot(taken, head_columns(rows, g), preferred_element_type=F32)
        if pairs > 1:
            pair_kv += prod[g]
        pair_kv = pair_kv.astype(BF16)
        for i in range(CHIP_BLOCKS):
            block = pair_kv[i * BLK : (i + 1) * BLK]
            kv[g, BACK + i, 0] = block[:, :HD]
            kv[g, BACK + i, 1] = block[:, HD:].T
        passed(0, g).start()

    local[1].wait()
    q_send.wait_recv()

    causal = (
        lax.broadcasted_iota(jnp.int32, (BLK, GROUP * BLK), 0)
        <= lax.broadcasted_iota(jnp.int32, (BLK, GROUP * BLK), 1) % BLK
    )

    def attend(i, g, low, high, own, old):
        rows = q[
            pl.ds(pl.multiple_of(i * BLK, BLK), BLK),
            pl.ds(pl.multiple_of(g * (GROUP * HD), GROUP * HD), GROUP * HD),
        ]
        heads = jnp.concatenate([rows[:, h * HD : (h + 1) * HD] for h in range(GROUP)], axis=0)
        tiles, offsets = [], []
        top = old
        for key in range(low, high):
            tile = lax.dot_general(kv[g, key, 0], heads, NT, preferred_element_type=F32)
            if own and key == high - 1:
                tile = jnp.where(causal, tile, -jnp.inf)
                offset = None
                highest = jnp.max(tile, axis=0, keepdims=True) * SCALE2
            else:
                offset = bias[i * BACK + key]
                highest = jnp.max(tile, axis=0, keepdims=True) * SCALE2 + offset
            tiles.append(tile)
            offsets.append(offset)
            top = highest if top is None else jnp.maximum(top, highest)
        total = None
        packed = []
        for tile, offset in zip(tiles, offsets):
            level = top if offset is None else top - offset
            weights = jnp.exp2(tile * SCALE2 - level)
            packed.append(weights.astype(BF16))
            amount = jnp.sum(weights, axis=0, keepdims=True)
            total = amount if total is None else total + amount
        values = jnp.concatenate([kv[g, key, 1] for key in range(low, high)], axis=1)
        summed = jnp.dot(values, jnp.concatenate(packed, axis=0), preferred_element_type=F32)
        return top, total, summed

    def join(i, g, low, high):
        old = m_s[i, g]
        top, total, summed = attend(i, g, low, high, False, old)
        keep = jnp.exp2(old - top)
        return top, total + l_s[i, g] * keep, summed + acc_s[i, g] * keep

    def finish(i, g, top, total, summed):
        result = (summed * (1.0 / total)).astype(BF16)
        lse = (top + jnp.log2(total)) * LN2
        for h in range(GROUP):
            o[g, i, :, h * HD : (h + 1) * HD] = result[:, h * BLK : (h + 1) * BLK].T
            lse_b[i, pl.ds(g * GROUP + h, 1), :] = lse[:, h * BLK : (h + 1) * BLK]

    def out_copy(i, g):
        rows = pl.ds((i % 2) * BLK, BLK)
        there = pl.ds(pl.multiple_of(core * HALF + g * (GROUP * HD), GROUP * HD), GROUP * HD)
        return o.at[g, i], out_ref.at[0, rows, there]

    def hand_out(i, g):
        src, dst = out_copy(i, g)

        @pl.when(core == i // 2)
        def _():
            pltpu.make_async_copy(src, dst, out_loc.at[i % 2, g]).start()

        @pl.when(core != i // 2)
        def _():
            remote(src, dst, out_send.at[i % 2, g], out_recv.at[i % 2, g], (x, partner)).start()

    last = CHIP_BLOCKS - 1

    for g in range(KVH // 2):
        for i in range(CHIP_BLOCKS):
            top, total, summed = attend(i, g, BACK, BACK + i + 1, True, None)
            acc_s[i, g] = summed
            m_s[i, g] = top
            l_s[i, g] = total

    for g in range(KVH // 2):
        passed(0, g).wait_recv()
        passed(1, g).start()

        @pl.loop(0, CHIP_BLOCKS)
        def _(i, g=g):
            top, total, summed = join(i, g, NEAR, BACK)
            acc_s[i, g] = summed
            m_s[i, g] = top
            l_s[i, g] = total

        finish(last, g, m_s[last, g], l_s[last, g], acc_s[last, g])
        hand_out(last, g)

    for g in range(KVH // 2):
        passed(1, g).wait_recv()
        for i in (2, 1, 0):
            finish(i, g, *join(i, g, i, NEAR))
            hand_out(i, g)

    for t in range(2):
        for j in range(2):
            slot_id = chip * CHIP_BLOCKS + t * 2 + j
            chosen = jnp.zeros((QH // 2, BLK), F32)
            for i in range(CHIP_BLOCKS):
                here = plan[0, chip * CHIP_BLOCKS + i] == slot_id
                chosen += jnp.where(here, jnp.float32(1.0), jnp.float32(0.0)) * lse_b[i]
            picked[t, :, pl.ds(j * BLK, BLK)] = chosen
    stat_rows = stats_ref.at[0, pl.ds(pl.multiple_of(core * (QH // 2), QH // 2), QH // 2)]
    keep_stats = pltpu.make_async_copy(picked.at[core], stat_rows, loc_sem.at[5])
    give_stats = remote(picked.at[other], stat_rows, st_send, st_recv, (x, partner))
    give_stats.start()
    keep_stats.start()

    for copy in piece_sends + sends:
        copy.wait_send()
    tok_send.wait_send()
    q_send.wait_send()

    @pl.when(dest_core != core)
    def _():
        piece_over.wait_send()

    for stage in range(2):
        for g in range(KVH // 2):
            passed(stage, g).wait_send()

    for i in range(CHIP_BLOCKS):
        for g in range(KVH // 2):
            src, dst = out_copy(i, g)

            @pl.when(core == i // 2)
            def _():
                pltpu.make_async_copy(src, dst, out_loc.at[i % 2, g]).wait()

            @pl.when(core != i // 2)
            def _():
                copy = remote(src, dst, out_send.at[i % 2, g], out_recv.at[i % 2, g], (x, partner))
                copy.wait_send()
                copy.wait_recv()

    keep_stats.wait()
    give_stats.wait_send()
    give_stats.wait_recv()


def body(n, tokens, queries, kv_weight, doc_blocks, block_mask, plan):
    wide = 64 * n * n
    hbm = pl.BlockSpec(memory_space=pltpu.HBM)
    dma = pltpu.SemaphoreType.DMA
    parts = KVH // 2
    rows = CHIP_BLOCKS * BLK
    gates = jnp.transpose(block_mask, (2, 0, 1))
    return pl.pallas_call(
        functools.partial(kernel, n),
        out_shape=(
            jax.ShapeDtypeStruct(queries.shape, BF16),
            jax.ShapeDtypeStruct((1, QH, tokens.shape[1]), F32),
        ),
        in_specs=[hbm] * 6,
        out_specs=(hbm, hbm),
        scratch_shapes=[
            pltpu.VMEM((rows, wide), BF16),
            pltpu.VMEM((n, n, 64, 2 * KW), BF16),
            pltpu.VMEM((rows, HALF), BF16),
            pltpu.VMEM((parts, WINDOW, 2, BLK, HD), BF16),
            pltpu.VMEM((parts, rows, 2 * HD), F32),
            pltpu.VMEM((parts, CHIP_BLOCKS, BLK, GROUP * HD), BF16),
            pltpu.VMEM((CHIP_BLOCKS, parts, HD, GROUP * BLK), F32),
            pltpu.VMEM((CHIP_BLOCKS, parts, 1, GROUP * BLK), F32),
            pltpu.VMEM((CHIP_BLOCKS, parts, 1, GROUP * BLK), F32),
            pltpu.VMEM((CHIP_BLOCKS, QH // 2, BLK), F32),
            pltpu.VMEM((2, QH // 2, 2 * BLK), F32),
            pltpu.SMEM(doc_blocks.shape, jnp.int32),
            pltpu.SMEM(gates.shape, jnp.int32),
            pltpu.SMEM(plan.shape, jnp.int32),
            pltpu.SMEM((CHIP_BLOCKS * MAXDOC,), F32),
            dma((6,)),
            dma((2,)),
            dma((2,)),
            dma((4,)),
            dma((4,)),
            dma((n,)),
            dma((n,)),
            dma((2, n // 2 + 1, 2)),
            dma((2, n // 2 + 1, 2)),
            dma((2, parts)),
            dma((2, parts)),
            dma((2, parts)),
            dma((2, parts)),
            dma((2, parts)),
            dma,
            dma,
        ],
        compiler_params=pltpu.CompilerParams(
            collective_id=0, has_side_effects=True, vmem_limit_bytes=60 * 1024 * 1024
        ),
    )(tokens, queries, kv_weight, doc_blocks, gates, plan)


def solution(mesh):
    in_specs = (
        P("dp", "ctx", None),
        P("dp", "ctx", None),
        P("ctx", "dp"),
        P("dp", None),
        P("dp", None, None),
        P("dp", None),
    )
    out_specs = (P("dp", "ctx", None), P("dp", None, "ctx"))
    n = math.isqrt(mesh.shape["ctx"] // 2)
    return jax.shard_map(
        functools.partial(body, n), mesh=mesh, in_specs=in_specs, out_specs=out_specs, check_vma=False
    )
```

```python
import functools
import math

import jax
import jax.numpy as jnp
from jax import lax
from jax.experimental import pallas as pl
from jax.experimental.pallas import tpu as pltpu
from jax.sharding import PartitionSpec as P

HD = 128
QH = 16
KVH = 4
BLK = 128
MAXDOC = 8
GROUP = QH // KVH
CHIP_BLOCKS = 4
BACK = MAXDOC - 1
WINDOW = BACK + CHIP_BLOCKS
NEAR = BACK - CHIP_BLOCKS
HALF = QH * HD // 2
KW = KVH * HD // 2
SCALE2 = math.log2(math.e) / math.sqrt(HD)
LN2 = math.log(2.0)
MESH = pl.DeviceIdType.MESH
BF16 = jnp.bfloat16
F32 = jnp.float32
NT = (((1,), (1,)), ((), ()))


def kernel(
    n,
    tok_in,
    q_in,
    w_in,
    docs_in,
    mask_in,
    plan_in,
    out_ref,
    stats_ref,
    tok,
    wbuf,
    q,
    kv,
    prod,
    o,
    acc_s,
    m_s,
    l_s,
    lse_b,
    picked,
    docs,
    mask,
    plan,
    bias,
    loc_sem,
    tok_sem,
    q_sem,
    wx_send,
    wx_recv,
    s1_send,
    s1_recv,
    s2_send,
    s2_recv,
    kv_send,
    kv_recv,
    out_loc,
    out_send,
    out_recv,
    st_send,
    st_recv,
):
    x = lax.axis_index("dp")
    ctx = lax.axis_index("ctx")
    chips = n * n
    half = n // 2
    core = lax.rem(ctx, 2)
    chip = lax.div(ctx, 2)
    z = lax.rem(chip, n)
    y = lax.div(chip, n)
    other = 1 - core
    partner = chip * 2 + other

    def by_core(zero, one):
        return zero + core * (one - zero)

    first_pos = by_core(y, z)
    ring_pos = by_core(z, y)

    def first_peer(step):
        pos = lax.rem(first_pos + step, n)
        return by_core(pos * n + z, y * n + pos) * 2 + core

    def ring_peer(step):
        pos = lax.rem(ring_pos + step, n)
        return by_core(y * n + pos, pos * n + z) * 2 + core

    after = lax.rem(chip + 1, chips) * 2 + core
    before = lax.rem(chip + chips - 1, chips) * 2 + core

    def remote(src, dst, send, recv, device):
        return pltpu.make_async_remote_copy(
            src_ref=src, dst_ref=dst, send_sem=send, recv_sem=recv, device_id=device, device_id_type=MESH
        )

    def arrived(ref, sem):
        pltpu.make_async_copy(ref, ref, sem).wait()

    barrier = pltpu.get_barrier_semaphore()
    peers = [(x, partner)]
    for step in range(1, 4):
        other_x = lax.rem(x + step, 4)
        peers += [(other_x, ctx), (other_x, partner)]
    peers += [(x, first_peer(step)) for step in range(1, n)]
    peers += [(x, ring_peer(1)), (x, ring_peer(n - 1)), (x, after), (x, before)]
    for peer in peers:
        pl.semaphore_signal(barrier, inc=1, device_id=peer, device_id_type=MESH)

    local = [
        pltpu.make_async_copy(tok_in.at[0], tok.at[pl.ds(core * 256, 256)], loc_sem.at[0]),
        pltpu.make_async_copy(
            q_in.at[0, :, pl.ds(pl.multiple_of(core * HALF, HALF), HALF)],
            q.at[pl.ds(core * 256, 256)],
            loc_sem.at[1],
        ),
    ]
    tables = [
        pltpu.make_async_copy(docs_in, docs, loc_sem.at[2]),
        pltpu.make_async_copy(mask_in, mask, loc_sem.at[3]),
        pltpu.make_async_copy(plan_in, plan, loc_sem.at[4]),
    ]
    pl.semaphore_wait(barrier, len(peers))

    dest_core = lax.rem(x, 2)
    part = lax.div(x, 2)
    dest_a = z + dest_core * (y - z)
    dest_b = y + dest_core * (z - y)
    slot = wbuf.at[
        dest_a,
        dest_b,
        pl.ds(pl.multiple_of(core * 32, 32), 32),
        pl.ds(pl.multiple_of(part * KW, KW), KW),
    ]
    place = part * 2 + core
    dest_ctx = chip * 2 + dest_core
    piece_sends = [
        remote(w_in, slot, wx_send.at[step], wx_recv.at[place], (lax.rem(x + step, 4), dest_ctx))
        for step in (2, 1, 3)
    ]
    for copy in piece_sends:
        copy.start()
    piece_over = remote(w_in, slot, wx_send.at[0], wx_recv.at[place], (x, partner))

    @pl.when(dest_core == core)
    def _():
        pltpu.make_async_copy(w_in, slot, wx_recv.at[place]).start()

    @pl.when(dest_core != core)
    def _():
        piece_over.start()

    for copy in tables + local:
        copy.start()

    tok_send = remote(
        tok_in.at[0], tok.at[pl.ds(core * 256, 256)], tok_sem.at[0], tok_sem.at[1], (x, partner)
    )
    q_send = remote(
        q_in.at[0, :, pl.ds(pl.multiple_of(other * HALF, HALF), HALF)],
        q.at[pl.ds(core * 256, 256)],
        q_sem.at[0],
        q_sem.at[1],
        (x, partner),
    )
    for k in range(4):
        arrived(
            wbuf.at[ring_pos, first_pos, pl.ds((k % 2) * 32, 32), pl.ds((k // 2) * KW, KW)],
            wx_recv.at[k],
        )

    steps = half

    def ring_copy(way, k, h):
        row = n - (k - 1) if way == 0 else k - 1
        chunk = wbuf.at[lax.rem(ring_pos + row, n), pl.ds(h * half, half)]
        to = ring_peer(1) if way == 0 else ring_peer(n - 1)
        return remote(chunk, chunk, s2_send.at[way, k, h], s2_recv.at[way, k, h], (x, to))

    def ring_got(way, k, h):
        row = n - k if way == 0 else k
        arrived(wbuf.at[lax.rem(ring_pos + row, n), pl.ds(h * half, half)], s2_recv.at[way, k, h])

    sends = []

    def start(copy):
        copy.start()
        sends.append(copy)

    def ring_start(way, k, h):
        if k < steps or h == way:
            start(ring_copy(way, k, h))

    def pair_operands(m):
        taken, rows = [], []
        for j in range(n):
            row = 2 * m + j // half
            pair = 2 * (j % half)
            rows.append(wbuf[by_core(2 * m, row), by_core(j, pair)])
            rows.append(wbuf[by_core(2 * m + 1, row), by_core(j, pair + 1)])
            column = by_core(j * n + 2 * m, row * n + pair) * 64
            taken.append(tok[:, pl.ds(pl.multiple_of(column, 128), 128)])
        rows = jnp.concatenate(rows, axis=0)
        return jnp.concatenate(taken, axis=1), rows

    def head_columns(rows, g):
        return jnp.concatenate(
            [rows[:, g * HD : (g + 1) * HD], rows[:, KW + g * HD : KW + (g + 1) * HD]], axis=1
        )

    def project(m, fresh):
        taken, rows = pair_operands(m)
        for g in range(KVH // 2):
            part_sum = jnp.dot(taken, head_columns(rows, g), preferred_element_type=F32)
            prod[g] = part_sum if fresh else prod[g] + part_sum

    pairs = half
    odd = lax.rem(ring_pos, 2)
    middle = lax.div(ring_pos, 2)
    near_side = (pairs - 1) - odd * (pairs - 2)
    far_side = 1 + odd * (pairs - 2)
    units = {
        4: [middle, lax.rem(middle + 1, pairs)],
        8: [
            middle,
            lax.rem(middle + near_side, pairs),
            lax.rem(middle + far_side, pairs),
            lax.rem(middle + 2, pairs),
        ],
    }[n]

    mine = wbuf.at[ring_pos, first_pos]
    for step in sorted(range(1, n), key=lambda step: -min(step, n - step)):
        start(remote(mine, mine, s1_send.at[step], s1_recv.at[step], (x, first_peer(step))))
    tok_send.start()
    q_send.start()

    for copy in tables:
        copy.wait()
    base = chip * CHIP_BLOCKS - BACK

    def count(j, state):
        end = state[0] + docs[0, j]
        return (end,) + tuple(
            state[1 + b] + jnp.where(base + b >= end, 1, 0) for b in range(WINDOW)
        )

    zero = jnp.int32(0)
    document = lax.fori_loop(0, docs.shape[1], count, (zero,) * (WINDOW + 1))[1:]
    for i in range(CHIP_BLOCKS):
        for s in range(BACK):
            key = i + s
            keep = jnp.logical_and(document[key] == document[i + BACK], base + key >= 0)
            gate = mask[BACK - s - 1, 0, chip * CHIP_BLOCKS + i] == 1
            keep = jnp.logical_and(keep, gate)
            bias[i * MAXDOC + s] = jnp.where(
                keep, jnp.float32(0.0), jnp.float32(-jnp.inf)
            )

    for step in range(1, n):
        source = lax.rem(first_pos + n - step, n)
        arrived(wbuf.at[ring_pos, source], s1_recv.at[step])

    order = ((0, 0), (1, 1), (0, 1), (1, 0))
    for k in range(1, steps + 1):
        for way, h in order:
            if k > 1:
                ring_got(way, k - 1, h)
            ring_start(way, k, h)
        if k > 1:
            if k == 2:
                local[0].wait()
                tok_send.wait_recv()
            project(units[k - 2], k == 2)
    ring_got(0, steps, 0)
    ring_got(1, steps, 1)
    def passed(stage, g):
        if stage == 0:
            src, dst, count = BACK, NEAR, CHIP_BLOCKS
        else:
            src, dst, count = NEAR + 1, 0, NEAR
        return remote(
            kv.at[g, pl.ds(src, count)],
            kv.at[g, pl.ds(dst, count)],
            kv_send.at[stage, g],
            kv_recv.at[stage, g],
            (x, after),
        )

    taken, rows = pair_operands(units[-1])
    for g in range(KVH // 2):
        pair_kv = jnp.dot(taken, head_columns(rows, g), preferred_element_type=F32)
        if pairs > 1:
            pair_kv += prod[g]
        pair_kv = pair_kv.astype(BF16)
        for i in range(CHIP_BLOCKS):
            block = pair_kv[i * BLK : (i + 1) * BLK]
            kv[g, BACK + i, 0] = block[:, :HD]
            kv[g, BACK + i, 1] = block[:, HD:].T
        passed(0, g).start()

    local[1].wait()
    q_send.wait_recv()

    causal = (
        lax.broadcasted_iota(jnp.int32, (BLK, GROUP * BLK), 0)
        <= lax.broadcasted_iota(jnp.int32, (BLK, GROUP * BLK), 1) % BLK
    )

    def attend(i, g, low, high, own, old):
        rows = q[
            pl.ds(pl.multiple_of(i * BLK, BLK), BLK),
            pl.ds(pl.multiple_of(g * (GROUP * HD), GROUP * HD), GROUP * HD),
        ]
        heads = jnp.concatenate([rows[:, h * HD : (h + 1) * HD] for h in range(GROUP)], axis=0)
        tiles, offsets = [], []
        top = old
        for key in range(low, high):
            tile = lax.dot_general(kv[g, key, 0], heads, NT, preferred_element_type=F32)
            if own and key == high - 1:
                tile = jnp.where(causal, tile, -jnp.inf)
                offset = None
                highest = jnp.max(tile, axis=0, keepdims=True) * SCALE2
            else:
                offset = bias[i * BACK + key]
                highest = jnp.max(tile, axis=0, keepdims=True) * SCALE2 + offset
            tiles.append(tile)
            offsets.append(offset)
            top = highest if top is None else jnp.maximum(top, highest)
        total = None
        packed = []
        for tile, offset in zip(tiles, offsets):
            level = top if offset is None else top - offset
            weights = jnp.exp2(tile * SCALE2 - level)
            packed.append(weights.astype(BF16))
            amount = jnp.sum(weights, axis=0, keepdims=True)
            total = amount if total is None else total + amount
        values = jnp.concatenate([kv[g, key, 1] for key in range(low, high)], axis=1)
        summed = jnp.dot(values, jnp.concatenate(packed, axis=0), preferred_element_type=F32)
        return top, total, summed

    def join(i, g, low, high):
        old = m_s[i, g]
        top, total, summed = attend(i, g, low, high, False, old)
        keep = jnp.exp2(old - top)
        return top, total + l_s[i, g] * keep, summed + acc_s[i, g] * keep

    def finish(i, g, top, total, summed):
        result = (summed * (1.0 / total)).astype(BF16)
        lse = (top + jnp.log2(total)) * LN2
        for h in range(GROUP):
            o[g, i, :, h * HD : (h + 1) * HD] = result[:, h * BLK : (h + 1) * BLK].T
            lse_b[i, pl.ds(g * GROUP + h, 1), :] = lse[:, h * BLK : (h + 1) * BLK]

    def out_copy(i, g):
        rows = pl.ds((i % 2) * BLK, BLK)
        there = pl.ds(pl.multiple_of(core * HALF + g * (GROUP * HD), GROUP * HD), GROUP * HD)
        return o.at[g, i], out_ref.at[0, rows, there]

    def hand_out(i, g):
        src, dst = out_copy(i, g)

        @pl.when(core == i // 2)
        def _():
            pltpu.make_async_copy(src, dst, out_loc.at[i % 2, g]).start()

        @pl.when(core != i // 2)
        def _():
            remote(src, dst, out_send.at[i % 2, g], out_recv.at[i % 2, g], (x, partner)).start()

    last = CHIP_BLOCKS - 1

    for g in range(KVH // 2):
        for i in range(CHIP_BLOCKS):
            top, total, summed = attend(i, g, BACK, BACK + i + 1, True, None)
            acc_s[i, g] = summed
            m_s[i, g] = top
            l_s[i, g] = total

    for g in range(KVH // 2):
        passed(0, g).wait_recv()
        passed(1, g).start()

        @pl.loop(0, CHIP_BLOCKS)
        def _(i, g=g):
            top, total, summed = join(i, g, NEAR, BACK)
            acc_s[i, g] = summed
            m_s[i, g] = top
            l_s[i, g] = total

        finish(last, g, m_s[last, g], l_s[last, g], acc_s[last, g])
        hand_out(last, g)

    for g in range(KVH // 2):
        passed(1, g).wait_recv()
        for i in (2, 1, 0):
            finish(i, g, *join(i, g, i, NEAR))
            hand_out(i, g)

    for t in range(2):
        for j in range(2):
            slot_id = chip * CHIP_BLOCKS + t * 2 + j
            chosen = jnp.zeros((QH // 2, BLK), F32)
            for i in range(CHIP_BLOCKS):
                here = plan[0, chip * CHIP_BLOCKS + i] == slot_id
                chosen += jnp.where(here, jnp.float32(1.0), jnp.float32(0.0)) * lse_b[i]
            picked[t, :, pl.ds(j * BLK, BLK)] = chosen
    stat_rows = stats_ref.at[0, pl.ds(pl.multiple_of(core * (QH // 2), QH // 2), QH // 2)]
    keep_stats = pltpu.make_async_copy(picked.at[core], stat_rows, loc_sem.at[5])
    give_stats = remote(picked.at[other], stat_rows, st_send, st_recv, (x, partner))
    give_stats.start()
    keep_stats.start()

    for copy in piece_sends + sends:
        copy.wait_send()
    tok_send.wait_send()
    q_send.wait_send()

    @pl.when(dest_core != core)
    def _():
        piece_over.wait_send()

    for stage in range(2):
        for g in range(KVH // 2):
            passed(stage, g).wait_send()

    for i in range(CHIP_BLOCKS):
        for g in range(KVH // 2):
            src, dst = out_copy(i, g)

            @pl.when(core == i // 2)
            def _():
                pltpu.make_async_copy(src, dst, out_loc.at[i % 2, g]).wait()

            @pl.when(core != i // 2)
            def _():
                copy = remote(src, dst, out_send.at[i % 2, g], out_recv.at[i % 2, g], (x, partner))
                copy.wait_send()
                copy.wait_recv()

    keep_stats.wait()
    give_stats.wait_send()
    give_stats.wait_recv()


def body(n, tokens, queries, kv_weight, doc_blocks, block_mask, plan):
    wide = 64 * n * n
    hbm = pl.BlockSpec(memory_space=pltpu.HBM)
    dma = pltpu.SemaphoreType.DMA
    parts = KVH // 2
    rows = CHIP_BLOCKS * BLK
    gates = jnp.transpose(block_mask, (2, 0, 1))
    return pl.pallas_call(
        functools.partial(kernel, n),
        out_shape=(
            jax.ShapeDtypeStruct(queries.shape, BF16),
            jax.ShapeDtypeStruct((1, QH, tokens.shape[1]), F32),
        ),
        in_specs=[hbm] * 6,
        out_specs=(hbm, hbm),
        scratch_shapes=[
            pltpu.VMEM((rows, wide), BF16),
            pltpu.VMEM((n, n, 64, 2 * KW), BF16),
            pltpu.VMEM((rows, HALF), BF16),
            pltpu.VMEM((parts, WINDOW, 2, BLK, HD), BF16),
            pltpu.VMEM((parts, rows, 2 * HD), F32),
            pltpu.VMEM((parts, CHIP_BLOCKS, BLK, GROUP * HD), BF16),
            pltpu.VMEM((CHIP_BLOCKS, parts, HD, GROUP * BLK), F32),
            pltpu.VMEM((CHIP_BLOCKS, parts, 1, GROUP * BLK), F32),
            pltpu.VMEM((CHIP_BLOCKS, parts, 1, GROUP * BLK), F32),
            pltpu.VMEM((CHIP_BLOCKS, QH // 2, BLK), F32),
            pltpu.VMEM((2, QH // 2, 2 * BLK), F32),
            pltpu.SMEM(doc_blocks.shape, jnp.int32),
            pltpu.SMEM(gates.shape, jnp.int32),
            pltpu.SMEM(plan.shape, jnp.int32),
            pltpu.SMEM((CHIP_BLOCKS * MAXDOC,), F32),
            dma((6,)),
            dma((2,)),
            dma((2,)),
            dma((4,)),
            dma((4,)),
            dma((n,)),
            dma((n,)),
            dma((2, n // 2 + 1, 2)),
            dma((2, n // 2 + 1, 2)),
            dma((2, parts)),
            dma((2, parts)),
            dma((2, parts)),
            dma((2, parts)),
            dma((2, parts)),
            dma,
            dma,
        ],
        compiler_params=pltpu.CompilerParams(
            collective_id=0, has_side_effects=True, vmem_limit_bytes=60 * 1024 * 1024
        ),
    )(tokens, queries, kv_weight, doc_blocks, gates, plan)


def solution(mesh):
    in_specs = (
        P("dp", "ctx", None),
        P("dp", "ctx", None),
        P("ctx", "dp"),
        P("dp", None),
        P("dp", None, None),
        P("dp", None),
    )
    out_specs = (P("dp", "ctx", None), P("dp", None, "ctx"))
    n = math.isqrt(mesh.shape["ctx"] // 2)
    return jax.shard_map(
        functools.partial(body, n), mesh=mesh, in_specs=in_specs, out_specs=out_specs, check_vma=False
    )
```
